32 devices in a mesh: src: 8 (over y, x, core), tgt: 4 (over z).
Axes of the slice: x: 2, y: 2, z: 4, core: 2. Of those that a mesh axis runs over, the one named last changes fastest.
Arguments:
- src_points: bfloat16 [64, 4096], P(None, ('src', 'tgt')), may hold values from -3 to 3
- tgt_points: bfloat16 [64, 1024], P(None, 'tgt'), may hold values from -3 to 3
- src_log_mass: float32 [4096], P(('src', 'tgt')), may hold values from -4 to 4
- tgt_log_mass: bfloat16 [1024], P('tgt'), may hold values from -4 to 4
- tgt_potential: bfloat16 [1024], P('tgt'), may hold values from -18 to 168
- src_cluster: int32 [4096], P(('src', 'tgt')), may hold values from 0 to 63, as said below
- tgt_cluster: int32 [1024], P('tgt'), may hold values from 0 to 63, as said below
- kept_pairs: int32 [1024, 2], replicated, may hold values from 0 to 63, as said below
Outputs:
- new_src_potential: float32 [4096], P(('src', 'tgt'))
- new_tgt_potential: float32 [1024], P('tgt')
The draws below stay inside these ranges and needn't reach their ends.
Inputs may be any that keep to these rules, and one draw needn't show every extreme that they name: `src_cluster`: never falls along the cells; every cluster holds at least one cell. `tgt_cluster`: never falls along the cells; every cluster holds at least one cell. `kept_pairs`: each pair stands once; every cluster of either day is in some pair.
All inputs are finite; a program needn't handle non-finite values.
Results may differ from the reference program's by a relative error of at most 0.00045.
Values may be sent and summed in bfloat16 or wider, within the bound.
No kernel may reach another device: no remote copies, remote signals or barrier semaphores. Data moves between devices by JAX's collectives and lax.ppermute only.
A program may use at most 128 MiB of HBM per device.

```python
import jax
import jax.numpy as jnp
from jax import lax

DIM = 64
CLUSTERS = 64
NPAIRS = 1024
S_DEV = 128
NS = 4096
NT = 1024


def sorted_labels(key, total_cells):
    weights = jax.random.randint(key, (CLUSTERS,), 1, 5).astype(jnp.int32)
    bounds = jnp.cumsum(weights) * total_cells // jnp.sum(weights)
    positions = jnp.arange(total_cells, dtype=jnp.int32)
    return jnp.sum((bounds[None, :-1] <= positions[:, None]).astype(jnp.int32), axis=1).astype(jnp.int32)


def draw_src_cluster(key, part):
    return sorted_labels(jax.random.fold_in(key, 11), NS)


def draw_tgt_cluster(key, part):
    return sorted_labels(jax.random.fold_in(key, 13), NT)


def draw_kept_pairs(key, part):
    base_key, lift_key = jax.random.split(jax.random.fold_in(key, 7))
    pair_index = jnp.arange(CLUSTERS * CLUSTERS, dtype=jnp.int32)
    src_side = pair_index // CLUSTERS
    tgt_side = pair_index % CLUSTERS
    cluster_lift = jax.random.randint(lift_key, (CLUSTERS,), 0, 4).astype(jnp.int32)
    base_score = jax.random.randint(base_key, (CLUSTERS * CLUSTERS,), 0, 32768).astype(jnp.int32)
    scores = base_score + cluster_lift[src_side] * 8192 + jnp.where(src_side == tgt_side, 131072, 0)
    scores = scores * 4096 + pair_index
    chosen_scores, chosen = lax.top_k(scores, NPAIRS)
    return jnp.stack([chosen // CLUSTERS, chosen % CLUSTERS], axis=1).astype(jnp.int32)


def draw_tgt_potential(key, part):
    values = jnp.clip(3.0 * jax.random.normal(key, (NT,), jnp.float32), -18.0, 18.0)
    return values.astype(jnp.bfloat16)


def block_scale(rng, dims, cuts, smallest, largest):
    def one(position, shards_of):
        steps = jax.random.uniform(jax.random.fold_in(jax.random.fold_in(rng, 6), position), (shards_of,), jnp.float32, smallest / len(cuts), largest / len(cuts))
        return jnp.repeat(jnp.exp(steps), dims[position] // shards_of).reshape((-1,) + (1,) * (len(dims) - position - 1))

    loudness = one(*cuts[0])
    for cut in cuts[1:]:
        loudness = loudness * one(*cut)
    return loudness


def gaussian(rng, extent, deviation, reach, pieces=(), held_as=jnp.bfloat16):
    level = block_scale(rng, extent, pieces, -0.22, 0.18) if pieces else 1.0
    values = jax.random.normal(rng, extent, jnp.float32) * deviation * level
    return jnp.minimum(jnp.maximum(values, -reach), reach).astype(held_as)


def setup_inputs(seed: int = 0) -> dict:
    seeds = jax.random.split(jax.random.key(seed), 9)
    src_points = gaussian(seeds[0], (DIM, NS), 0.5, 3.0, ((1, 32),))
    tgt_points = gaussian(seeds[1], (DIM, NT), 0.5, 3.0, ((1, 4),))
    src_log_mass = gaussian(seeds[2], (NS,), 1.0, 4.0, ((0, 32),), jnp.float32)
    tgt_log_mass = gaussian(seeds[3], (NT,), 1.0, 4.0, ((0, 4),))
    tgt_potential = draw_tgt_potential(jax.random.fold_in(seeds[8], 71), 0)
    src_cluster = draw_src_cluster(jax.random.fold_in(seeds[8], 71), 0)
    tgt_cluster = draw_tgt_cluster(jax.random.fold_in(seeds[8], 71), 0)
    kept_pairs = draw_kept_pairs(jax.random.fold_in(seeds[8], 71), 0)
    return {"src_points": src_points, "tgt_points": tgt_points, "src_log_mass": src_log_mass, "tgt_log_mass": tgt_log_mass, "tgt_potential": tgt_potential, "src_cluster": src_cluster, "tgt_cluster": tgt_cluster, "kept_pairs": kept_pairs}


FLOOR_VALUE = -1.0e30
EPSILON = 1.0
MASS_FACTOR = 10.0 / 11.0


def square_norms(points):
    widened = points.astype(jnp.float32)
    return jnp.sum(widened * widened, axis=0)


def build_grid(kept_pairs, labels):
    src_side = (kept_pairs[:, 0][:, None] == labels[None, :]).astype(jnp.float32)
    tgt_side = (kept_pairs[:, 1][:, None] == labels[None, :]).astype(jnp.float32)
    return jnp.dot(src_side.T, tgt_side, preferred_element_type=jnp.float32)


def combine_pairs(earlier, later):
    highest = jnp.maximum(earlier[0], later[0])
    return highest, earlier[1] * jnp.exp(earlier[0] - highest) + later[1] * jnp.exp(later[0] - highest)


def reference(src_points, tgt_points, src_log_mass, tgt_log_mass, tgt_potential, src_cluster, tgt_cluster, kept_pairs):
    labels = jnp.arange(CLUSTERS, dtype=jnp.int32)
    pair_grid = build_grid(kept_pairs, labels)
    tgt_wide = tgt_points.astype(jnp.float32)
    tgt_norms = square_norms(tgt_points)
    tgt_onehot = (labels[:, None] == tgt_cluster[None, :]).astype(jnp.float32)
    row_bias = (tgt_potential.astype(jnp.float32) - tgt_norms) / EPSILON + tgt_log_mass.astype(jnp.float32)
    block_count = NS // S_DEV
    block_points = src_points.reshape(DIM, block_count, S_DEV).transpose(1, 0, 2)
    block_labels = src_cluster.reshape(block_count, S_DEV)
    block_mass = src_log_mass.reshape(block_count, S_DEV)

    def shared(points, clusters):
        sq_norms = square_norms(points)
        src_onehot = (clusters[:, None] == labels[None, :]).astype(jnp.float32)
        row_grid = jnp.dot(src_onehot, pair_grid, preferred_element_type=jnp.float32)
        kept_mask = jnp.dot(row_grid, tgt_onehot, preferred_element_type=jnp.float32) > 0.5
        crossed = jnp.dot(points.astype(jnp.float32).T, tgt_wide, preferred_element_type=jnp.float32, precision=lax.Precision.HIGHEST)
        return sq_norms, kept_mask, crossed

    def row_block(inputs):
        points, clusters = inputs
        sq_norms, kept_mask, crossed = shared(points, clusters)
        scores = row_bias[None, :] - (sq_norms[:, None] - 2.0 * crossed) / EPSILON
        scores = jnp.where(kept_mask, scores, FLOOR_VALUE)
        highest = jnp.max(scores, axis=1)
        totals = jnp.sum(jnp.where(kept_mask, jnp.exp(scores - highest[:, None]), 0.0), axis=1)
        return -MASS_FACTOR * EPSILON * (highest + jnp.log(totals))

    new_src = lax.map(row_block, (block_points, block_labels))

    def column_block(running, inputs):
        points, clusters, potential, masses = inputs
        sq_norms, kept_mask, crossed = shared(points, clusters)
        col_bias = (potential - sq_norms) / EPSILON + masses
        scores = col_bias[:, None] - (tgt_norms[None, :] - 2.0 * crossed) / EPSILON
        scores = jnp.where(kept_mask, scores, FLOOR_VALUE)
        highest = jnp.max(scores, axis=0)
        totals = jnp.sum(jnp.where(kept_mask, jnp.exp(scores - highest[None, :]), 0.0), axis=0)
        return combine_pairs(running, (highest, totals)), highest

    start_state = (jnp.full((NT,), FLOOR_VALUE, jnp.float32), jnp.zeros((NT,), jnp.float32))
    final_state, ignored = lax.scan(column_block, start_state, (block_points, block_labels, new_src, block_mass))
    new_tgt = -MASS_FACTOR * EPSILON * (final_state[0] + jnp.log(final_state[1]))
    return new_src.reshape(NS), new_tgt
```

```python
import functools

import jax
import jax.numpy as jnp
from jax import lax
from jax.experimental import pallas as pl
from jax.experimental.pallas import tpu as pltpu
from jax.sharding import PartitionSpec as P

CLUSTERS = 64
EPSILON = 1.0
MASS_FACTOR = 10.0 / 11.0
BARRED = -(2.0**100)
TERMS = 8
SMALL, LARGE = 4 << 20, 32 << 20

F32, BF16 = jnp.float32, jnp.bfloat16


def in_three(value):
    high = value.astype(BF16).astype(F32)
    rest = value - high
    middle = rest.astype(BF16).astype(F32)
    return high, middle, rest - middle


def square_norms(points):
    widened = points.astype(F32)
    return jnp.sum(widened * widened, axis=0, keepdims=True)


def pack_kernel(
    src_hbm, tgt_hbm, src_mass_hbm, tgt_mass_hbm, potential_hbm, src_label_hbm, tgt_label_hbm,
    packed_ref,
    src_ref, tgt_ref, src_mass_ref, tgt_mass_ref, potential_ref, src_label_ref, tgt_label_ref, sems,
):
    pairs = (
        (tgt_hbm, tgt_ref),
        (src_hbm, src_ref),
        (src_mass_hbm, src_mass_ref),
        (tgt_mass_hbm, tgt_mass_ref),
        (potential_hbm, potential_ref),
        (src_label_hbm, src_label_ref),
        (tgt_label_hbm, tgt_label_ref),
    )
    copies = [pltpu.make_async_copy(a, b, sems.at[n]) for n, (a, b) in enumerate(pairs)]
    for copy in copies:
        copy.start()
    for copy in copies:
        copy.wait()
    dim, rows = src_ref.shape
    columns = tgt_ref.shape[1]
    fold = columns // rows
    slab = dim // fold
    targets = tgt_ref[...]
    sources = src_ref[...]
    packed_ref[0:dim, :] = targets
    for part in range(fold):
        packed_ref[dim : dim + slab, part * rows : (part + 1) * rows] = sources[
            part * slab : (part + 1) * slab
        ]
    tgt_mass = tgt_mass_ref[...].astype(F32).reshape(1, columns)
    potential = potential_ref[...].astype(F32).reshape(1, columns)
    row_bias = (potential - square_norms(targets)) / EPSILON + tgt_mass
    tgt_label = tgt_label_ref[...].astype(F32).reshape(1, columns)
    src_norms = square_norms(sources)
    src_rest = src_mass_ref[...].reshape(1, rows) - src_norms / EPSILON
    src_label = src_label_ref[...].astype(F32).reshape(1, rows)
    lines = [*in_three(row_bias), tgt_label]
    narrow = [src_label, *in_three(src_norms), *in_three(src_rest)]
    narrow += [jnp.zeros((1, rows), F32)] * (-len(narrow) % fold)
    for start in range(0, len(narrow), fold):
        lines.append(jnp.concatenate(narrow[start : start + fold], axis=1))
    place = lax.broadcasted_iota(jnp.int32, (TERMS, columns), 0)
    terms = jnp.zeros((TERMS, columns), F32)
    for number, line in enumerate(lines):
        terms = jnp.where(place == number, line, terms)
    packed_ref[dim + slab : dim + slab + TERMS, :] = terms.astype(BF16)


def grid_kernel(pairs_ref, grid_ref):
    count = pairs_ref.shape[1]
    names = lax.broadcasted_iota(jnp.int32, (CLUSTERS, count), 0)
    src_side = (names == pairs_ref[0:1, :]).astype(F32).astype(BF16)
    tgt_side = (names == pairs_ref[1:2, :]).astype(F32).astype(BF16)
    grid = lax.dot_general(
        tgt_side, src_side, (((1,), (1,)), ((), ())), preferred_element_type=F32
    )
    grid_ref[...] = grid.astype(BF16)


def main_kernel(dim, rows, columns, spread, grid_ref, *refs):
    blocks, (new_src_hbm, share_ref, new_src_ref, sem) = refs[:-4], refs[-4:]
    leave = pltpu.make_async_copy(new_src_ref, new_src_hbm, sem)
    fold = columns // rows
    slab = dim // fold
    names_rows = lax.broadcasted_iota(jnp.int32, (CLUSTERS, rows), 0).astype(F32)
    names_columns = lax.broadcasted_iota(jnp.int32, (CLUSTERS, columns), 0).astype(F32)
    place = lax.broadcasted_iota(jnp.int32, (TERMS, 2 * 128), 0)
    half = lax.broadcasted_iota(jnp.int32, (TERMS, 2 * 128), 1) < 128
    picked = jnp.where(
        half, (place < 3).astype(F32), ((place >= 3) & (place < 6)).astype(F32)
    ).astype(BF16)
    left, right, biases, norms, rests = [], [], [], [], []
    for block in blocks:
        terms = block[dim + slab :, :].astype(F32)
        biases.append(terms[0:1] + terms[1:2] + terms[2:3])
        tgt_onehot = (names_columns == terms[3:4]).astype(F32).astype(BF16)
        right.append(jnp.concatenate([block[0:dim, :], tgt_onehot], axis=0))
        narrow = [
            terms[4 + n // fold : 5 + n // fold, (n % fold) * rows : (n % fold + 1) * rows]
            for n in range(7)
        ]
        src_onehot = (names_rows == narrow[0]).astype(F32).astype(BF16)
        kept = jnp.dot(grid_ref[...], src_onehot, preferred_element_type=F32)
        penalty = ((1.0 - kept) * BARRED).astype(BF16)
        sources = jnp.concatenate(
            [
                block[dim : dim + slab, part * rows : (part + 1) * rows].astype(F32)
                for part in range(fold)
            ],
            axis=0,
        )
        left.append(jnp.concatenate([(2.0 / EPSILON * sources).astype(BF16), penalty], axis=0))
        side_place = lax.broadcasted_iota(jnp.int32, (TERMS, rows), 0)
        side = jnp.zeros((TERMS, rows), F32)
        for n in range(6):
            side = jnp.where(side_place == n, narrow[n + 1], side)
        both = lax.dot_general(
            side.astype(BF16), picked, (((0,), (0,)), ((), ())), preferred_element_type=F32
        )
        norms.append(both[:, 0:1])
        rests.append(both[:, 128:129])
    own_norms = square_norms(blocks[0][0:dim, :])
    own_scores, col_biases = [], []
    for number in range(len(blocks)):
        scores = [
            lax.dot_general(
                left[number], side, (((0,), (0,)), ((), ())), preferred_element_type=F32
            )
            for side in right
        ]
        own_scores.append(scores[0])
        biased = [score + bias for score, bias in zip(scores, biases, strict=True)]
        highest = functools.reduce(jnp.maximum, [jnp.max(b, 1, keepdims=True) for b in biased])
        total = sum(jnp.sum(jnp.exp(b - highest), 1, keepdims=True) for b in biased)
        norm = norms[number]
        new_src = -MASS_FACTOR * EPSILON * (highest + jnp.log(total) - norm / EPSILON)
        col_biases.append(new_src / EPSILON + rests[number])
        if number == 0:
            wide = jnp.broadcast_to(new_src, (rows, 128))
            new_src_ref[...] = wide.T[0:1, :]
            leave.start()
    shifted = [score + bias for score, bias in zip(own_scores, col_biases, strict=True)]
    peak = functools.reduce(jnp.maximum, [jnp.max(s, 0, keepdims=True) for s in shifted])
    mass = sum(jnp.sum(jnp.exp(s - peak), 0, keepdims=True) for s in shifted)
    share = peak + jnp.log(mass) - own_norms / EPSILON
    share_ref[...] = jnp.broadcast_to(share[None], (spread, 1, columns))
    leave.wait()


def tail_kernel(shares_ref, new_tgt_ref):
    shares = shares_ref[...][:, 0, :]
    peak = jnp.max(shares, axis=0, keepdims=True)
    total = jnp.sum(jnp.exp(shares - peak), axis=0, keepdims=True)
    new_tgt_ref[...] = -MASS_FACTOR * EPSILON * (peak + jnp.log(total))


def vmem(count):
    return [pl.BlockSpec(memory_space=pltpu.VMEM)] * count


def partners(count):
    if count & (count - 1) == 0:
        return [[(i, i ^ k) for i in range(count)] for k in range(1, count)]
    return [[(i, (i + k) % count) for i in range(count)] for k in range(1, count)]


def solution(mesh):
    src_size, tgt_size = mesh.shape["src"], mesh.shape["tgt"]

    def body(
        src_points, tgt_points, src_log_mass, tgt_log_mass, tgt_potential, src_cluster, tgt_cluster,
        kept_pairs,
    ):
        dim, rows = src_points.shape
        columns = tgt_points.shape[1]
        height = dim + dim * rows // columns + TERMS
        arrays = (
            src_points, tgt_points, src_log_mass, tgt_log_mass, tgt_potential, src_cluster,
            tgt_cluster,
        )
        packed = pl.pallas_call(
            pack_kernel,
            out_shape=jax.ShapeDtypeStruct((height, columns), BF16),
            in_specs=[pl.BlockSpec(memory_space=pltpu.HBM)] * len(arrays),
            out_specs=vmem(1)[0],
            scratch_shapes=[pltpu.VMEM(a.shape, a.dtype) for a in arrays]
            + [pltpu.SemaphoreType.DMA((len(arrays),))],
            name="pack",
            compiler_params=pltpu.CompilerParams(vmem_limit_bytes=SMALL),
        )(*[pltpu.with_memory_space_constraint(a, pltpu.HBM) for a in arrays])
        others = [lax.ppermute(packed, "tgt", pairs) for pairs in partners(tgt_size)]
        grid = pl.pallas_call(
            grid_kernel,
            out_shape=jax.ShapeDtypeStruct((CLUSTERS, CLUSTERS), BF16),
            in_specs=vmem(1),
            out_specs=vmem(1)[0],
            name="grid",
            compiler_params=pltpu.CompilerParams(vmem_limit_bytes=SMALL),
        )(kept_pairs.T)
        new_src, share = pl.pallas_call(
            functools.partial(main_kernel, dim, rows, columns, src_size),
            out_shape=(
                jax.ShapeDtypeStruct((1, rows), F32),
                jax.ShapeDtypeStruct((src_size, 1, columns), F32),
            ),
            in_specs=vmem(1 + tgt_size),
            out_specs=(pl.BlockSpec(memory_space=pltpu.HBM), vmem(1)[0]),
            scratch_shapes=[pltpu.VMEM((1, rows), F32), pltpu.SemaphoreType.DMA],
            name="halves",
            compiler_params=pltpu.CompilerParams(vmem_limit_bytes=LARGE),
        )(grid, packed, *others)
        shares = lax.all_to_all(share, "src", split_axis=0, concat_axis=0, tiled=True)
        new_tgt = pl.pallas_call(
            tail_kernel,
            out_shape=jax.ShapeDtypeStruct((1, columns), F32),
            in_specs=vmem(1),
            out_specs=vmem(1)[0],
            name="tail",
            compiler_params=pltpu.CompilerParams(vmem_limit_bytes=SMALL),
        )(shares)
        return new_src.reshape(rows), new_tgt.reshape(columns)

    in_specs = (
        P(None, ("src", "tgt")),
        P(None, "tgt"),
        P(("src", "tgt")),
        P("tgt"),
        P("tgt"),
        P(("src", "tgt")),
        P("tgt"),
        P(),
    )
    out_specs = (P(("src", "tgt")), P("tgt"))
    return jax.shard_map(body, mesh=mesh, in_specs=in_specs, out_specs=out_specs, check_vma=False)
```
